32 devices in a mesh: group: 4 (over z), member: 8 (over y, x, core).
Axes of the slice: x: 2, y: 2, z: 4, core: 2. Of those that a mesh axis runs over, the one named last changes fastest.
Arguments:
- embeddings: bfloat16 [24576, 1024], P(('group', 'member')), may hold values from -18 to 18
- prior: float32 [24576, 1000], P(('group', 'member')), may hold values from 0.05 to 5
- source_member: int32 [4, 8, 4], P('group'), may hold values from 0 to 7, as said below
- source_block: int32 [4, 8, 4], P('group'), may hold values from 0 to 5
- cross_block: int32 [4, 8, 2], P(None, 'member'), may hold values from 0 to 5
- row_links: int32 [24576, 4], P(('group', 'member')), may hold values from 0 to 5
Outputs:
- propagated: float32 [24576, 1000], P(('group', 'member'))
The draws below stay inside these ranges and needn't reach their ends.
Inputs may be any that keep to these rules, and one draw needn't show every extreme that they name: `source_member`: no device names itself, and the members in one device's list are distinct. Over all lists of one group no member is named more than 7 times, and in every group some member is named exactly 7 times.
All inputs are finite; a program needn't handle non-finite values.
Results may differ from the reference program's by a relative error of at most 0.0079.
Values may be sent and summed in bfloat16 or wider, within the bound.
A program may use at most 64 MiB of HBM per device.

```python
import math
import jax
import jax.numpy as jnp
from jax import lax

D = 1024
C = 1000
ROWS_DEV = 768
BR = 128
IN_SLOTS = 4
CROSS = 2
SERVE_CAP = 7
LINKS = 4
ITERS = 2
BLOCKS_DEV = 6
SLOTS = 6
TOTAL = 24576
N_GROUP = 4
N_MEMBER = 8


def link_table(key):
    return jax.random.randint(jax.random.fold_in(key, 31), (TOTAL, LINKS), 0, SLOTS).astype(jnp.int32)


def draw_row_links(key, part):
    return link_table(key)


def draw_embeddings(key, part):
    return jnp.clip(jax.random.normal(key, (TOTAL, D), jnp.float32), -6.0, 6.0).astype(jnp.bfloat16)


def arranged(subkey):
    order = jax.random.permutation(subkey, N_MEMBER).astype(jnp.int32)
    positions = jnp.arange(N_MEMBER, dtype=jnp.int32)
    offsets = jnp.arange(1, IN_SLOTS + 1, dtype=jnp.int32)
    at_position = order[(positions[:, None] + offsets[None, :]) % N_MEMBER]
    redirect = (positions[:, None] >= 1) & (positions[:, None] <= SERVE_CAP - IN_SLOTS) & (offsets[None, :] == 1)
    at_position = jnp.where(redirect, order[0], at_position)
    return jnp.zeros((N_MEMBER, IN_SLOTS), jnp.int32).at[order].set(at_position)


def draw_source_member(key, part):
    subkeys = jax.random.split(jax.random.fold_in(key, 21), N_GROUP)
    return jax.vmap(arranged)(subkeys).astype(jnp.int32)


def place_ends(values, stream_key, smallest, largest):
    extent = values.shape
    place = [jax.random.randint(jax.random.fold_in(stream_key, axis), (), 0, extent[axis]) for axis in range(len(extent))]
    values = values.at[tuple(place)].set(smallest)
    longest = extent.index(max(extent))
    place[longest] = (place[longest] + 1) % extent[longest]
    return values.at[tuple(place)].set(largest)


def steps_of(rng, dims, cuts, least, largest):
    factor_of = 1.0
    for axis_at, blocks in cuts:
        draws = jax.random.uniform(jax.random.fold_in(jax.random.fold_in(rng, 6), axis_at), (blocks,), jnp.float32, least / len(cuts), largest / len(cuts))
        factor_of = factor_of * jnp.repeat(jnp.exp(draws), dims[axis_at] // blocks).reshape((-1,) + (1,) * (len(dims) - 1 - axis_at))
    return factor_of


def setup_inputs(seed: int = 0) -> dict:
    streams_of = jax.random.split(jax.random.key(seed), 7)
    return {
        "embeddings": draw_embeddings(jax.random.fold_in(streams_of[6], 71), 0),
        "prior": jnp.clip(jnp.exp(math.log(5.0) - 4.6051702 * jax.random.uniform(streams_of[1], (TOTAL, C), jnp.float32) ** steps_of(streams_of[1], (TOTAL, C), ((0, 32),), -0.2, 0.2)), 0.05, 5.0),
        "source_member": draw_source_member(jax.random.fold_in(streams_of[6], 71), 0),
        "source_block": place_ends(jax.random.randint(streams_of[3], (N_GROUP, N_MEMBER, IN_SLOTS), 0, BLOCKS_DEV), jax.random.fold_in(streams_of[3], 1), 0, BLOCKS_DEV - 1).astype(jnp.int32),
        "cross_block": place_ends(jax.random.randint(streams_of[4], (N_GROUP, N_MEMBER, CROSS), 0, BLOCKS_DEV), jax.random.fold_in(streams_of[4], 1), 0, BLOCKS_DEV - 1).astype(jnp.int32),
        "row_links": draw_row_links(jax.random.fold_in(streams_of[6], 71), 0),
    }


MIXING = 0.8


def allowed_mask(row_links):
    slot_ids = jnp.arange(SLOTS, dtype=jnp.int32)
    slot_hits = jnp.any(row_links[:, :, None] == slot_ids[None, None, :], axis=1)
    neighbour_mask = jnp.repeat(slot_hits, BR, axis=1)
    local_mask = jnp.logical_not(jnp.eye(ROWS_DEV, dtype=bool))
    return jnp.concatenate([local_mask, neighbour_mask], axis=1)


def kernel_weights(queries, key_rows, allowed):
    scores = jnp.dot(queries, key_rows.T, preferred_element_type=jnp.float32) * (D ** -0.5)
    scores = jnp.where(allowed, scores, -jnp.inf)
    highest = jnp.max(scores, axis=1, keepdims=True)
    powers = jnp.where(allowed, jnp.exp(scores - highest), 0.0)
    return (powers / jnp.sum(powers, axis=1, keepdims=True)).astype(jnp.bfloat16)


def sharpen(weights, key_labels, prior_share):
    mixed = MIXING * jnp.dot(weights, key_labels, preferred_element_type=jnp.float32) + (1.0 - MIXING) * prior_share
    squared = mixed * mixed
    return squared / jnp.sum(squared, axis=1, keepdims=True)


def collect(blocks_all, device, members, block_ids, cross_ids):
    group_index = device // N_MEMBER
    member_index = device % N_MEMBER
    inner = blocks_all[group_index * N_MEMBER + members, block_ids]
    below_device = ((group_index + N_GROUP - 1) % N_GROUP) * N_MEMBER + member_index
    above_device = ((group_index + 1) % N_GROUP) * N_MEMBER + member_index
    outer = blocks_all[jnp.stack([below_device, above_device]).astype(jnp.int32), cross_ids]
    lane_count = blocks_all.shape[-1]
    return jnp.concatenate([inner.reshape(-1, lane_count), outer.reshape(-1, lane_count)], axis=0)


def reference(embeddings, prior, source_member, source_block, cross_block, row_links):
    devices = N_GROUP * N_MEMBER
    emb_blocks = embeddings.reshape(devices, ROWS_DEV // BR, BR, D)
    prior_share = prior / jnp.sum(prior, axis=1, keepdims=True)
    labels = prior_share.astype(jnp.bfloat16)
    device_ids = jnp.arange(devices, dtype=jnp.int32)
    emb_dev = embeddings.reshape(devices, ROWS_DEV, D)
    share_dev = prior_share.reshape(devices, ROWS_DEV, C)
    links_dev = row_links.reshape(devices, ROWS_DEV, LINKS)
    members_dev = source_member.reshape(devices, IN_SLOTS)
    blocks_dev = source_block.reshape(devices, IN_SLOTS)
    cross_dev = cross_block.reshape(devices, CROSS)
    result = prior_share
    for iteration in range(ITERS):
        lab_blocks = labels.reshape(devices, ROWS_DEV // BR, BR, C)
        lab_dev = labels.reshape(devices, ROWS_DEV, C)

        def one_device(items):
            device, queries, own_labels, share_rows, links, members, block_ids, cross_ids = items
            key_rows = jnp.concatenate([queries, collect(emb_blocks, device, members, block_ids, cross_ids)], axis=0)
            key_labels = jnp.concatenate([own_labels, collect(lab_blocks, device, members, block_ids, cross_ids)], axis=0)
            weights = kernel_weights(queries, key_rows, allowed_mask(links))
            return sharpen(weights, key_labels, share_rows)

        result = lax.map(one_device, (device_ids, emb_dev, lab_dev, share_dev, links_dev, members_dev, blocks_dev, cross_dev))
        result = result.reshape(devices * ROWS_DEV, C)
        labels = result.astype(jnp.bfloat16)
    return result * C
```

```python
import functools

import jax
import jax.numpy as jnp
from jax import lax
from jax.experimental import pallas as pl
from jax.experimental.pallas import tpu as pltpu
from jax.sharding import PartitionSpec as P

BR = 128
SERVE_CAP = 7
ITERS = 2


MIXING = 0.8


def extended(value, sides, width):
    for axis, dim in sides:
        size, length = (lax.axis_size(axis), value.shape[dim])
        up = [(i, (i + 1) % size) for i in range(size)]
        down = [(j, i) for i, j in up]
        last = lax.slice_in_dim(value, length - width, length, axis=dim)
        first = lax.slice_in_dim(value, 0, width, axis=dim)
        before = lax.ppermute(last, axis, up)
        after = lax.ppermute(first, axis, down)
        value = jnp.concatenate([before, value, after], axis=dim)
    return value


def allowed_mask(row_links, near_total, slot_total, row_count, block_rows):
    slot_ids = jnp.arange(slot_total, dtype=jnp.int32)
    slot_hits = jnp.any(row_links[:, :, None] == slot_ids[None, None, :], axis=1)
    near_mask = jnp.tile(slot_hits[:, :near_total], (1, block_rows))
    far_mask = jnp.repeat(slot_hits[:, near_total:], block_rows, axis=1)
    row_ids = lax.broadcasted_iota(jnp.int32, (row_count, row_count), 0)
    col_ids = lax.broadcasted_iota(jnp.int32, (row_count, row_count), 1)
    local_mask = row_ids != col_ids
    return jnp.concatenate([local_mask, near_mask, far_mask], axis=1)


def kernel_weights(queries, key_rows, allowed):
    features = queries.shape[1]
    scores = lax.dot_general(
        queries, key_rows, (((1,), (1,)), ((), ())), preferred_element_type=jnp.float32
    )
    scores = scores * features ** (-0.5)
    scores = jnp.where(allowed, scores, -jnp.inf)
    highest = jnp.max(scores, axis=1, keepdims=True)
    powers = jnp.where(allowed, jnp.exp(scores - highest), 0.0)
    return (powers / jnp.sum(powers, axis=1, keepdims=True)).astype(jnp.bfloat16)


def sharpen(weights, key_labels, prior_share):
    mixed = (
        MIXING * jnp.dot(weights, key_labels, preferred_element_type=jnp.float32)
        + (1.0 - MIXING) * prior_share
    )
    squared = mixed * mixed
    return squared / jnp.sum(squared, axis=1, keepdims=True)


def near_keys(delivered):
    return delivered.reshape(-1, delivered.shape[-1])


def far_keys(padded):
    return jnp.concatenate([padded[0], padded[-1]], axis=0)


def relay_body(embeddings, prior, source_member, source_block, cross_block, row_links):
    member_count = lax.axis_size("member")
    group_count = lax.axis_size("group")
    group_index = lax.axis_index("group")
    member_index = lax.axis_index("member")
    row_count, features = embeddings.shape
    classes = prior.shape[1]
    block_rows = BR
    block_count = row_count // block_rows
    piece_rows = block_rows // member_count
    owners = source_member[0]
    slot_count = owners.shape[1]
    flat_owner = owners.reshape(-1)
    flat_block = source_block[0].reshape(-1)
    order_ids = jnp.arange(flat_owner.shape[0], dtype=jnp.int32)
    earlier = (flat_owner[:, None] == flat_owner[None, :]) & (
        order_ids[None, :] < order_ids[:, None]
    )
    rank_ids = jnp.sum(earlier.astype(jnp.int32), axis=1)
    serve_ids = jnp.arange(SERVE_CAP, dtype=jnp.int32)
    serving = (flat_owner[None, :] == member_index) & (rank_ids[None, :] == serve_ids[:, None])
    served_blocks = jnp.sum(jnp.where(serving, flat_block[None, :], 0), axis=1)
    relay_member = lax.broadcasted_iota(jnp.int32, (member_count, piece_rows, SERVE_CAP), 0)
    relay_row = lax.broadcasted_iota(jnp.int32, (member_count, piece_rows, SERVE_CAP), 1)
    relay_rows = (
        served_blocks[None, None, :] * block_rows + relay_member * piece_rows + relay_row
    ).reshape(-1)
    owner_grid = owners.reshape(member_count, 1, slot_count)
    rank_grid = rank_ids.reshape(member_count, 1, slot_count)
    piece_grid = lax.broadcasted_iota(jnp.int32, (member_count, piece_rows, slot_count), 1)
    deliver_rows = (
        owner_grid * (piece_rows * SERVE_CAP) + piece_grid * SERVE_CAP + rank_grid
    ).reshape(-1)
    below_group = (group_index + group_count - 1) % group_count
    above_group = (group_index + 1) % group_count
    cross_pick = jnp.stack([cross_block[below_group, 0, 1], cross_block[above_group, 0, 0]])
    allowed = allowed_mask(
        row_links, slot_count, slot_count + cross_block.shape[2], row_count, block_rows
    )
    prior_share = prior / jnp.sum(prior, axis=1, keepdims=True)
    labels = prior_share.astype(jnp.bfloat16)
    emb_blocks = embeddings.reshape(block_count, block_rows, features)

    def relay_pieces(flat_rows):
        return jnp.take(flat_rows, relay_rows, axis=0).reshape(
            member_count, piece_rows, SERVE_CAP, flat_rows.shape[-1]
        )

    def deliver_pieces(received):
        lane_count = received.shape[-1]
        picked = jnp.take(received.reshape(-1, lane_count), deliver_rows, axis=0)
        return picked.reshape(member_count, piece_rows, slot_count, lane_count)

    result = prior_share
    emb_relay = lax.all_to_all(
        relay_pieces(embeddings), "member", split_axis=0, concat_axis=0, tiled=True
    )
    emb_near = lax.all_to_all(
        deliver_pieces(emb_relay), "member", split_axis=0, concat_axis=0, tiled=True
    )
    emb_far = extended(emb_blocks[cross_pick], (("group", 0),), 1)
    key_rows = jnp.concatenate([embeddings, near_keys(emb_near), far_keys(emb_far)], axis=0)
    weights = kernel_weights(embeddings, key_rows, allowed)
    for iteration in range(ITERS):
        lab_blocks = labels.reshape(block_count, block_rows, classes)
        lab_relay = lax.all_to_all(
            relay_pieces(labels), "member", split_axis=0, concat_axis=0, tiled=True
        )
        lab_near = lax.all_to_all(
            deliver_pieces(lab_relay), "member", split_axis=0, concat_axis=0, tiled=True
        )
        lab_far = extended(lab_blocks[cross_pick], (("group", 0),), 1)
        key_labels = jnp.concatenate([labels, near_keys(lab_near), far_keys(lab_far)], axis=0)
        result = sharpen(weights, key_labels, prior_share)
        labels = result.astype(jnp.bfloat16)
    return result * classes


MESH = pl.DeviceIdType.MESH


def partner_of(member, mask, member_count):
    bit = 1
    while bit < member_count:
        if mask & bit:
            member = member + bit - 2 * bit * (member // bit % 2)
        bit *= 2
    return member


def same(left, right):
    gap = left - right
    return 1 - jnp.minimum(gap * gap, 1)


def direct_kernel(
    member_count, group_count,
    owners, blocks, cross, emb_hbm, prior_hbm, links_hbm, out_hbm,
    emb, share, links, emb_send, emb_recv, lab, lab_send, lab_recv, scores, weights, mix, out,
    load_sem, store_sem, send_sem, recv_sem,
):
    group = lax.axis_index("group")
    me = lax.axis_index("member")
    block_count, _, features = emb.shape
    rows = block_count * BR
    in_slots = owners.shape[0]
    below = (group + group_count - 1) % group_count
    above = (group + 1) % group_count
    group_blocks = 2 if block_count % 2 == 0 else 1
    width = group_blocks * BR
    chunks = rows // width
    slots = 2 + member_count - 1
    partners = [partner_of(me, mask, member_count) for mask in range(1, member_count)]
    targets = [(above, me), (below, me)] + [(group, p) for p in partners]
    sending = list(range(slots - 1, 1, -1)) + [0, 1]

    def lanes_of(c):
        return pl.ds(pl.multiple_of(c * width, width), width)

    emb_load = pltpu.make_async_copy(emb_hbm, emb, load_sem.at[0])
    prior_load = pltpu.make_async_copy(prior_hbm, share, load_sem.at[1])
    links_load = pltpu.make_async_copy(links_hbm, links, load_sem.at[2])
    emb_load.start()
    prior_load.start()
    links_load.start()

    barrier = pltpu.get_barrier_semaphore()
    for target in targets:
        pl.semaphore_signal(barrier, inc=1, device_id=target, device_id_type=MESH)

    picks = [cross[0, above], cross[1, below]]
    names = [jnp.int32(in_slots), jnp.int32(in_slots + 1)]
    for p in partners:
        pick = jnp.int32(0)
        name = jnp.int32(-1)
        for k in range(in_slots):
            pick += same(owners[k, p], me) * blocks[k, p]
            name += same(owners[k, me], p) * (k + 1)
        picks.append(pick)
        names.append(name)

    def copy_of(stage, s):
        src = emb_send.at[s] if stage == 0 else lab_send.at[stage - 1, s]
        dst = emb_recv.at[s] if stage == 0 else lab_recv.at[stage - 1, s]
        return pltpu.make_async_remote_copy(
            src_ref=src, dst_ref=dst,
            send_sem=send_sem.at[stage, s], recv_sem=recv_sem.at[stage, s],
            device_id=targets[s], device_id_type=MESH,
        )

    emb_load.wait()
    pl.semaphore_wait(barrier, slots)
    for s in sending:
        emb_send[s] = emb[picks[s]]
        copy_of(0, s).start()

    def put_labels(c, value):
        value = value.astype(jnp.bfloat16)
        for b in range(group_blocks):
            lab[c * group_blocks + b] = value[:, b * BR:(b + 1) * BR]

    def send_labels(stage):
        for s in sending:
            lab_send[stage - 1, s] = lab[picks[s]]
            copy_of(stage, s).start()

    prior_load.wait()

    def first_labels(c, _):
        lanes = lanes_of(c)
        value = share[:, lanes]
        value = value / jnp.sum(value, axis=0, keepdims=True)
        put_labels(c, value)
        share[:, lanes] = value
        return _

    lax.fori_loop(0, chunks, first_labels, 0)
    send_labels(1)
    links_load.wait()

    def score_of(keys):
        value = lax.dot_general(
            keys, emb[...].reshape(rows, features), (((1,), (1,)), ((), ())), preferred_element_type=jnp.float32
        )
        return value * features ** (-0.5)

    def own_scores(b, _):
        span = pl.ds(pl.multiple_of(b * BR, BR), BR)
        value = score_of(emb[b])
        key_ids = lax.broadcasted_iota(jnp.int32, (BR, rows), 0) + b * BR
        row_ids = lax.broadcasted_iota(jnp.int32, (BR, rows), 1)
        scores[span, :] = jnp.where(key_ids != row_ids, value, -jnp.inf)
        return _

    lax.fori_loop(0, rows // BR, own_scores, 0)
    for s in range(slots):
        bias = jnp.max(jnp.where(links[...] == names[s], 0.0, -jnp.inf), axis=0, keepdims=True)
        copy_of(0, s).wait_recv()
        scores[rows + s * BR:rows + (s + 1) * BR, :] = score_of(emb_recv[s]) + bias

    def soften(b, _):
        lanes = pl.ds(pl.multiple_of(b * BR, BR), BR)
        value = scores[:, lanes]
        powers = jnp.exp(value - jnp.max(value, axis=0, keepdims=True))
        total = jnp.sum(powers, axis=0, keepdims=True)
        weights[:, lanes] = (powers * (1.0 / total)).astype(jnp.bfloat16)
        return _

    lax.fori_loop(0, rows // BR, soften, 0)

    def own_mix(c, _):
        lanes = lanes_of(c)
        keys = jnp.concatenate([lab[b] for b in range(block_count)], axis=1)
        mix[:, lanes] = jnp.dot(
            keys, weights[:rows, lanes], preferred_element_type=jnp.float32
        )
        return _

    def sharp_of(total, lanes):
        mixed = MIXING * total + (1.0 - MIXING) * share[:, lanes]
        squared = mixed * mixed
        return squared / jnp.sum(squared, axis=0, keepdims=True)

    spans = [(0, 3)] + [(s, min(s + 2, slots)) for s in range(3, slots, 2)]

    for stage in (1, 2):
        lax.fori_loop(0, chunks, own_mix, 0)
        for first, last in spans:
            for s in range(first, last):
                copy_of(stage, s).wait_recv()

            def arrived(c, _, first=first, last=last):
                lanes = lanes_of(c)
                keys = [lab_recv[stage - 1, s] for s in range(first, last)]
                keys = jnp.concatenate(keys, axis=1) if len(keys) > 1 else keys[0]
                total = mix[:, lanes] + jnp.dot(
                    keys, weights[rows + first * BR:rows + last * BR, lanes],
                    preferred_element_type=jnp.float32,
                )
                if last < slots:
                    mix[:, lanes] = total
                elif stage == 1:
                    put_labels(c, sharp_of(total, lanes))
                else:
                    out[:, lanes] = sharp_of(total, lanes)
                return _

            lax.fori_loop(0, chunks, arrived, 0)
        if stage == 1:
            send_labels(2)
    store = pltpu.make_async_copy(out, out_hbm, store_sem)
    store.start()
    for stage in range(ITERS + 1):
        for s in range(slots):
            copy_of(stage, s).wait_send()
    store.wait()


def direct_body(embeddings, prior, source_member, source_block, cross_block, row_links):
    member_count = lax.axis_size("member")
    group_count = lax.axis_size("group")
    rows, features = embeddings.shape
    classes = prior.shape[1]
    slots = 2 + member_count - 1
    keys = rows + slots * BR
    any_space = pl.BlockSpec(memory_space=pl.ANY)
    smem = pl.BlockSpec(memory_space=pltpu.SMEM)
    bf16, f32 = jnp.bfloat16, jnp.float32
    sharp = pl.pallas_call(
        functools.partial(direct_kernel, member_count, group_count),
        out_shape=jax.ShapeDtypeStruct((classes, rows), f32),
        in_specs=[smem] * 3 + [any_space] * 3,
        out_specs=any_space,
        scratch_shapes=[
            pltpu.VMEM((rows // BR, BR, features), bf16),
            pltpu.VMEM((classes, rows), f32),
            pltpu.VMEM((row_links.shape[1], rows), jnp.int32),
            pltpu.VMEM((slots, BR, features), bf16),
            pltpu.VMEM((slots, BR, features), bf16),
            pltpu.VMEM((rows // BR, classes, BR), bf16),
            pltpu.VMEM((ITERS, slots, classes, BR), bf16),
            pltpu.VMEM((ITERS, slots, classes, BR), bf16),
            pltpu.VMEM((keys, rows), f32),
            pltpu.VMEM((keys, rows), bf16),
            pltpu.VMEM((classes, rows), f32),
            pltpu.VMEM((classes, rows), f32),
            pltpu.SemaphoreType.DMA((3,)),
            pltpu.SemaphoreType.DMA,
            pltpu.SemaphoreType.DMA((ITERS + 1, slots)),
            pltpu.SemaphoreType.DMA((ITERS + 1, slots)),
        ],
        compiler_params=pltpu.CompilerParams(
            collective_id=0, has_side_effects=True, vmem_limit_bytes=60 * 2**20
        ),
    )(
        source_member[0].T, source_block[0].T, cross_block[:, 0, :].T,
        embeddings.reshape(rows // BR, BR, features), prior.T, row_links.T,
    )
    return sharp.T * classes


def solution(mesh):
    member_count = mesh.shape["member"]
    direct = member_count & (member_count - 1) == 0 and member_count - 1 <= SERVE_CAP
    body = direct_body if direct else relay_body
    placed = (
        P(("group", "member"), None),
        P(("group", "member"), None),
        P("group", None, None),
        P("group", None, None),
        P(None, "member", None),
        P(("group", "member"), None),
    )
    return jax.shard_map(
        body, mesh=mesh, in_specs=placed, out_specs=P(("group", "member"), None), check_vma=False
    )
```

```python
import functools

import jax
import jax.numpy as jnp
from jax import lax
from jax.experimental import pallas as pl
from jax.experimental.pallas import tpu as pltpu
from jax.sharding import PartitionSpec as P

BR = 128
SERVE_CAP = 7
ITERS = 2


MIXING = 0.8


def extended(value, sides, width):
    for axis, dim in sides:
        size, length = (lax.axis_size(axis), value.shape[dim])
        up = [(i, (i + 1) % size) for i in range(size)]
        down = [(j, i) for i, j in up]
        last = lax.slice_in_dim(value, length - width, length, axis=dim)
        first = lax.slice_in_dim(value, 0, width, axis=dim)
        before = lax.ppermute(last, axis, up)
        after = lax.ppermute(first, axis, down)
        value = jnp.concatenate([before, value, after], axis=dim)
    return value


def allowed_mask(row_links, near_total, slot_total, row_count, block_rows):
    slot_ids = jnp.arange(slot_total, dtype=jnp.int32)
    slot_hits = jnp.any(row_links[:, :, None] == slot_ids[None, None, :], axis=1)
    near_mask = jnp.tile(slot_hits[:, :near_total], (1, block_rows))
    far_mask = jnp.repeat(slot_hits[:, near_total:], block_rows, axis=1)
    row_ids = lax.broadcasted_iota(jnp.int32, (row_count, row_count), 0)
    col_ids = lax.broadcasted_iota(jnp.int32, (row_count, row_count), 1)
    local_mask = row_ids != col_ids
    return jnp.concatenate([local_mask, near_mask, far_mask], axis=1)


def kernel_weights(queries, key_rows, allowed):
    features = queries.shape[1]
    scores = lax.dot_general(
        queries, key_rows, (((1,), (1,)), ((), ())), preferred_element_type=jnp.float32
    )
    scores = scores * features ** (-0.5)
    scores = jnp.where(allowed, scores, -jnp.inf)
    highest = jnp.max(scores, axis=1, keepdims=True)
    powers = jnp.where(allowed, jnp.exp(scores - highest), 0.0)
    return (powers / jnp.sum(powers, axis=1, keepdims=True)).astype(jnp.bfloat16)


def sharpen(weights, key_labels, prior_share):
    mixed = (
        MIXING * jnp.dot(weights, key_labels, preferred_element_type=jnp.float32)
        + (1.0 - MIXING) * prior_share
    )
    squared = mixed * mixed
    return squared / jnp.sum(squared, axis=1, keepdims=True)


def near_keys(delivered):
    return delivered.reshape(-1, delivered.shape[-1])


def far_keys(padded):
    return jnp.concatenate([padded[0], padded[-1]], axis=0)


def relay_body(embeddings, prior, source_member, source_block, cross_block, row_links):
    member_count = lax.axis_size("member")
    group_count = lax.axis_size("group")
    group_index = lax.axis_index("group")
    member_index = lax.axis_index("member")
    row_count, features = embeddings.shape
    classes = prior.shape[1]
    block_rows = BR
    block_count = row_count // block_rows
    piece_rows = block_rows // member_count
    owners = source_member[0]
    slot_count = owners.shape[1]
    flat_owner = owners.reshape(-1)
    flat_block = source_block[0].reshape(-1)
    order_ids = jnp.arange(flat_owner.shape[0], dtype=jnp.int32)
    earlier = (flat_owner[:, None] == flat_owner[None, :]) & (
        order_ids[None, :] < order_ids[:, None]
    )
    rank_ids = jnp.sum(earlier.astype(jnp.int32), axis=1)
    serve_ids = jnp.arange(SERVE_CAP, dtype=jnp.int32)
    serving = (flat_owner[None, :] == member_index) & (rank_ids[None, :] == serve_ids[:, None])
    served_blocks = jnp.sum(jnp.where(serving, flat_block[None, :], 0), axis=1)
    relay_member = lax.broadcasted_iota(jnp.int32, (member_count, piece_rows, SERVE_CAP), 0)
    relay_row = lax.broadcasted_iota(jnp.int32, (member_count, piece_rows, SERVE_CAP), 1)
    relay_rows = (
        served_blocks[None, None, :] * block_rows + relay_member * piece_rows + relay_row
    ).reshape(-1)
    owner_grid = owners.reshape(member_count, 1, slot_count)
    rank_grid = rank_ids.reshape(member_count, 1, slot_count)
    piece_grid = lax.broadcasted_iota(jnp.int32, (member_count, piece_rows, slot_count), 1)
    deliver_rows = (
        owner_grid * (piece_rows * SERVE_CAP) + piece_grid * SERVE_CAP + rank_grid
    ).reshape(-1)
    below_group = (group_index + group_count - 1) % group_count
    above_group = (group_index + 1) % group_count
    cross_pick = jnp.stack([cross_block[below_group, 0, 1], cross_block[above_group, 0, 0]])
    allowed = allowed_mask(
        row_links, slot_count, slot_count + cross_block.shape[2], row_count, block_rows
    )
    prior_share = prior / jnp.sum(prior, axis=1, keepdims=True)
    labels = prior_share.astype(jnp.bfloat16)
    emb_blocks = embeddings.reshape(block_count, block_rows, features)

    def relay_pieces(flat_rows):
        return jnp.take(flat_rows, relay_rows, axis=0).reshape(
            member_count, piece_rows, SERVE_CAP, flat_rows.shape[-1]
        )

    def deliver_pieces(received):
        lane_count = received.shape[-1]
        picked = jnp.take(received.reshape(-1, lane_count), deliver_rows, axis=0)
        return picked.reshape(member_count, piece_rows, slot_count, lane_count)

    result = prior_share
    emb_relay = lax.all_to_all(
        relay_pieces(embeddings), "member", split_axis=0, concat_axis=0, tiled=True
    )
    emb_near = lax.all_to_all(
        deliver_pieces(emb_relay), "member", split_axis=0, concat_axis=0, tiled=True
    )
    emb_far = extended(emb_blocks[cross_pick], (("group", 0),), 1)
    key_rows = jnp.concatenate([embeddings, near_keys(emb_near), far_keys(emb_far)], axis=0)
    weights = kernel_weights(embeddings, key_rows, allowed)
    for iteration in range(ITERS):
        lab_blocks = labels.reshape(block_count, block_rows, classes)
        lab_relay = lax.all_to_all(
            relay_pieces(labels), "member", split_axis=0, concat_axis=0, tiled=True
        )
        lab_near = lax.all_to_all(
            deliver_pieces(lab_relay), "member", split_axis=0, concat_axis=0, tiled=True
        )
        lab_far = extended(lab_blocks[cross_pick], (("group", 0),), 1)
        key_labels = jnp.concatenate([labels, near_keys(lab_near), far_keys(lab_far)], axis=0)
        result = sharpen(weights, key_labels, prior_share)
        labels = result.astype(jnp.bfloat16)
    return result * classes


MESH = pl.DeviceIdType.MESH


def partner_of(member, mask, member_count):
    bit = 1
    while bit < member_count:
        if mask & bit:
            member = member + bit - 2 * bit * (member // bit % 2)
        bit *= 2
    return member


def same(left, right):
    gap = left - right
    return 1 - jnp.minimum(gap * gap, 1)


def direct_kernel(
    member_count, group_count,
    owners, blocks, cross, emb_hbm, prior_hbm, links_hbm, out,
    emb, share, links, emb_send, emb_recv, lab, lab_send, lab_recv, scores, weights, mix,
    load_sem, send_sem, recv_sem,
):
    group = lax.axis_index("group")
    me = lax.axis_index("member")
    block_count, _, features = emb.shape
    rows = block_count * BR
    in_slots = owners.shape[0]
    below = (group + group_count - 1) % group_count
    above = (group + 1) % group_count
    group_blocks = 2 if block_count % 2 == 0 else 1
    width = group_blocks * BR
    chunks = rows // width
    slots = 2 + member_count - 1
    partners = [partner_of(me, mask, member_count) for mask in range(1, member_count)]
    targets = [(above, me), (below, me)] + [(group, p) for p in partners]
    masks = sorted(range(1, member_count), key=lambda mask: (mask == 1, (mask >> 1).bit_count(), mask & 1))
    sending = [1 + mask for mask in masks] + [0, 1]

    def lanes_of(c):
        return pl.ds(pl.multiple_of(c * width, width), width)

    emb_load = pltpu.make_async_copy(emb_hbm, emb, load_sem.at[0])
    prior_load = pltpu.make_async_copy(prior_hbm, share, load_sem.at[1])
    links_load = pltpu.make_async_copy(links_hbm, links, load_sem.at[2])
    emb_load.start()
    prior_load.start()
    links_load.start()

    barrier = pltpu.get_barrier_semaphore()
    for target in targets:
        pl.semaphore_signal(barrier, inc=1, device_id=target, device_id_type=MESH)

    picks = [cross[0, above], cross[1, below]]
    names = [jnp.int32(in_slots), jnp.int32(in_slots + 1)]
    for p in partners:
        pick = jnp.int32(0)
        name = jnp.int32(-1)
        for k in range(in_slots):
            pick += same(owners[k, p], me) * blocks[k, p]
            name += same(owners[k, me], p) * (k + 1)
        picks.append(pick)
        names.append(name)

    def copy_of(stage, s):
        src = emb_send.at[s] if stage == 0 else lab_send.at[stage - 1, s]
        dst = emb_recv.at[s] if stage == 0 else lab_recv.at[stage - 1, s]
        return pltpu.make_async_remote_copy(
            src_ref=src, dst_ref=dst,
            send_sem=send_sem.at[stage, s], recv_sem=recv_sem.at[stage, s],
            device_id=targets[s], device_id_type=MESH,
        )

    emb_load.wait()
    pl.semaphore_wait(barrier, slots)
    for s in sending:
        emb_send[s] = emb[picks[s]]
        copy_of(0, s).start()

    def put_labels(c, value):
        value = value.astype(jnp.bfloat16)
        for b in range(group_blocks):
            lab[c * group_blocks + b] = value[:, b * BR:(b + 1) * BR]

    def send_labels(stage):
        for s in sending:
            lab_send[stage - 1, s] = lab[picks[s]]
            copy_of(stage, s).start()

    prior_load.wait()

    def first_labels(c, _):
        lanes = lanes_of(c)
        value = share[:, lanes]
        value = value / jnp.sum(value, axis=0, keepdims=True)
        put_labels(c, value)
        share[:, lanes] = value
        return _

    lax.fori_loop(0, chunks, first_labels, 0)
    send_labels(1)
    links_load.wait()

    def score_of(keys):
        value = lax.dot_general(
            keys, emb[...].reshape(rows, features), (((1,), (1,)), ((), ())), preferred_element_type=jnp.float32
        )
        return value * features ** (-0.5)

    def own_scores(b, _):
        span = pl.ds(pl.multiple_of(b * BR, BR), BR)
        value = score_of(emb[b])
        key_ids = lax.broadcasted_iota(jnp.int32, (BR, rows), 0) + b * BR
        row_ids = lax.broadcasted_iota(jnp.int32, (BR, rows), 1)
        scores[span, :] = jnp.where(key_ids != row_ids, value, -jnp.inf)
        return _

    lax.fori_loop(0, rows // BR, own_scores, 0)
    for s in range(slots):
        bias = jnp.max(jnp.where(links[...] == names[s], 0.0, -jnp.inf), axis=0, keepdims=True)
        copy_of(0, s).wait_recv()
        scores[rows + s * BR:rows + (s + 1) * BR, :] = score_of(emb_recv[s]) + bias

    def soften(b, _):
        lanes = pl.ds(pl.multiple_of(b * BR, BR), BR)
        value = scores[:, lanes]
        powers = jnp.exp(value - jnp.max(value, axis=0, keepdims=True))
        total = jnp.sum(powers, axis=0, keepdims=True)
        weights[:, lanes] = (powers * (1.0 / total)).astype(jnp.bfloat16)
        return _

    lax.fori_loop(0, rows // BR, soften, 0)

    def own_mix(c, _):
        lanes = lanes_of(c)
        keys = jnp.concatenate([lab[b] for b in range(block_count)], axis=1)
        mix[:, lanes] = jnp.dot(
            keys, weights[:rows, lanes], preferred_element_type=jnp.float32
        )
        return _

    def sharp_of(total, lanes):
        mixed = MIXING * total + (1.0 - MIXING) * share[:, lanes]
        squared = mixed * mixed
        return squared / jnp.sum(squared, axis=0, keepdims=True)

    spans = [(0, 3)] + [(s, min(s + 2, slots)) for s in range(3, slots, 2)]

    for stage in (1, 2):
        lax.fori_loop(0, chunks, own_mix, 0)
        for first, last in spans:
            for s in range(first, last):
                copy_of(stage, s).wait_recv()

            def arrived(c, _, first=first, last=last):
                lanes = lanes_of(c)
                keys = [lab_recv[stage - 1, s] for s in range(first, last)]
                keys = jnp.concatenate(keys, axis=1) if len(keys) > 1 else keys[0]
                total = mix[:, lanes] + jnp.dot(
                    keys, weights[rows + first * BR:rows + last * BR, lanes],
                    preferred_element_type=jnp.float32,
                )
                if last < slots:
                    mix[:, lanes] = total
                elif stage == 1:
                    put_labels(c, sharp_of(total, lanes))
                else:
                    out[:, lanes] = sharp_of(total, lanes)
                return _

            lax.fori_loop(0, chunks, arrived, 0)
        if stage == 1:
            send_labels(2)
    for stage in range(ITERS + 1):
        for s in range(slots):
            copy_of(stage, s).wait_send()


def direct_body(embeddings, prior, source_member, source_block, cross_block, row_links):
    member_count = lax.axis_size("member")
    group_count = lax.axis_size("group")
    rows, features = embeddings.shape
    classes = prior.shape[1]
    slots = 2 + member_count - 1
    keys = rows + slots * BR
    any_space = pl.BlockSpec(memory_space=pl.ANY)
    smem = pl.BlockSpec(memory_space=pltpu.SMEM)
    bf16, f32 = jnp.bfloat16, jnp.float32
    sharp = pl.pallas_call(
        functools.partial(direct_kernel, member_count, group_count),
        out_shape=pltpu.VMEM((classes, rows), f32),
        in_specs=[smem] * 3 + [any_space] * 3,
        out_specs=pl.BlockSpec(memory_space=pltpu.VMEM),
        scratch_shapes=[
            pltpu.VMEM((rows // BR, BR, features), bf16),
            pltpu.VMEM((classes, rows), f32),
            pltpu.VMEM((row_links.shape[1], rows), jnp.int32),
            pltpu.VMEM((slots, BR, features), bf16),
            pltpu.VMEM((slots, BR, features), bf16),
            pltpu.VMEM((rows // BR, classes, BR), bf16),
            pltpu.VMEM((ITERS, slots, classes, BR), bf16),
            pltpu.VMEM((ITERS, slots, classes, BR), bf16),
            pltpu.VMEM((keys, rows), f32),
            pltpu.VMEM((keys, rows), bf16),
            pltpu.VMEM((classes, rows), f32),
            pltpu.SemaphoreType.DMA((3,)),
            pltpu.SemaphoreType.DMA((ITERS + 1, slots)),
            pltpu.SemaphoreType.DMA((ITERS + 1, slots)),
        ],
        compiler_params=pltpu.CompilerParams(
            collective_id=0, has_side_effects=True, vmem_limit_bytes=60 * 2**20
        ),
    )(
        source_member[0].T, source_block[0].T, cross_block[:, 0, :].T,
        embeddings.reshape(rows // BR, BR, features), prior.T, row_links.T,
    )
    return sharp.T * classes


def solution(mesh):
    member_count = mesh.shape["member"]
    direct = member_count & (member_count - 1) == 0 and member_count - 1 <= SERVE_CAP
    body = direct_body if direct else relay_body
    placed = (
        P(("group", "member"), None),
        P(("group", "member"), None),
        P("group", None, None),
        P("group", None, None),
        P(None, "member", None),
        P(("group", "member"), None),
    )
    return jax.shard_map(
        body, mesh=mesh, in_specs=placed, out_specs=P(("group", "member"), None), check_vma=False
    )
```

```python
import functools

import jax
import jax.numpy as jnp
from jax import lax
from jax.experimental import pallas as pl
from jax.experimental.pallas import tpu as pltpu
from jax.sharding import PartitionSpec as P

BR = 128
SERVE_CAP = 7
ITERS = 2


MIXING = 0.8


def extended(value, sides, width):
    for axis, dim in sides:
        size, length = (lax.axis_size(axis), value.shape[dim])
        up = [(i, (i + 1) % size) for i in range(size)]
        down = [(j, i) for i, j in up]
        last = lax.slice_in_dim(value, length - width, length, axis=dim)
        first = lax.slice_in_dim(value, 0, width, axis=dim)
        before = lax.ppermute(last, axis, up)
        after = lax.ppermute(first, axis, down)
        value = jnp.concatenate([before, value, after], axis=dim)
    return value


def allowed_mask(row_links, near_total, slot_total, row_count, block_rows):
    slot_ids = jnp.arange(slot_total, dtype=jnp.int32)
    slot_hits = jnp.any(row_links[:, :, None] == slot_ids[None, None, :], axis=1)
    near_mask = jnp.tile(slot_hits[:, :near_total], (1, block_rows))
    far_mask = jnp.repeat(slot_hits[:, near_total:], block_rows, axis=1)
    row_ids = lax.broadcasted_iota(jnp.int32, (row_count, row_count), 0)
    col_ids = lax.broadcasted_iota(jnp.int32, (row_count, row_count), 1)
    local_mask = row_ids != col_ids
    return jnp.concatenate([local_mask, near_mask, far_mask], axis=1)


def kernel_weights(queries, key_rows, allowed):
    features = queries.shape[1]
    scores = lax.dot_general(
        queries, key_rows, (((1,), (1,)), ((), ())), preferred_element_type=jnp.float32
    )
    scores = scores * features ** (-0.5)
    scores = jnp.where(allowed, scores, -jnp.inf)
    highest = jnp.max(scores, axis=1, keepdims=True)
    powers = jnp.where(allowed, jnp.exp(scores - highest), 0.0)
    return (powers / jnp.sum(powers, axis=1, keepdims=True)).astype(jnp.bfloat16)


def sharpen(weights, key_labels, prior_share):
    mixed = (
        MIXING * jnp.dot(weights, key_labels, preferred_element_type=jnp.float32)
        + (1.0 - MIXING) * prior_share
    )
    squared = mixed * mixed
    return squared / jnp.sum(squared, axis=1, keepdims=True)


def near_keys(delivered):
    return delivered.reshape(-1, delivered.shape[-1])


def far_keys(padded):
    return jnp.concatenate([padded[0], padded[-1]], axis=0)


def relay_body(embeddings, prior, source_member, source_block, cross_block, row_links):
    member_count = lax.axis_size("member")
    group_count = lax.axis_size("group")
    group_index = lax.axis_index("group")
    member_index = lax.axis_index("member")
    row_count, features = embeddings.shape
    classes = prior.shape[1]
    block_rows = BR
    block_count = row_count // block_rows
    piece_rows = block_rows // member_count
    owners = source_member[0]
    slot_count = owners.shape[1]
    flat_owner = owners.reshape(-1)
    flat_block = source_block[0].reshape(-1)
    order_ids = jnp.arange(flat_owner.shape[0], dtype=jnp.int32)
    earlier = (flat_owner[:, None] == flat_owner[None, :]) & (
        order_ids[None, :] < order_ids[:, None]
    )
    rank_ids = jnp.sum(earlier.astype(jnp.int32), axis=1)
    serve_ids = jnp.arange(SERVE_CAP, dtype=jnp.int32)
    serving = (flat_owner[None, :] == member_index) & (rank_ids[None, :] == serve_ids[:, None])
    served_blocks = jnp.sum(jnp.where(serving, flat_block[None, :], 0), axis=1)
    relay_member = lax.broadcasted_iota(jnp.int32, (member_count, piece_rows, SERVE_CAP), 0)
    relay_row = lax.broadcasted_iota(jnp.int32, (member_count, piece_rows, SERVE_CAP), 1)
    relay_rows = (
        served_blocks[None, None, :] * block_rows + relay_member * piece_rows + relay_row
    ).reshape(-1)
    owner_grid = owners.reshape(member_count, 1, slot_count)
    rank_grid = rank_ids.reshape(member_count, 1, slot_count)
    piece_grid = lax.broadcasted_iota(jnp.int32, (member_count, piece_rows, slot_count), 1)
    deliver_rows = (
        owner_grid * (piece_rows * SERVE_CAP) + piece_grid * SERVE_CAP + rank_grid
    ).reshape(-1)
    below_group = (group_index + group_count - 1) % group_count
    above_group = (group_index + 1) % group_count
    cross_pick = jnp.stack([cross_block[below_group, 0, 1], cross_block[above_group, 0, 0]])
    allowed = allowed_mask(
        row_links, slot_count, slot_count + cross_block.shape[2], row_count, block_rows
    )
    prior_share = prior / jnp.sum(prior, axis=1, keepdims=True)
    labels = prior_share.astype(jnp.bfloat16)
    emb_blocks = embeddings.reshape(block_count, block_rows, features)

    def relay_pieces(flat_rows):
        return jnp.take(flat_rows, relay_rows, axis=0).reshape(
            member_count, piece_rows, SERVE_CAP, flat_rows.shape[-1]
        )

    def deliver_pieces(received):
        lane_count = received.shape[-1]
        picked = jnp.take(received.reshape(-1, lane_count), deliver_rows, axis=0)
        return picked.reshape(member_count, piece_rows, slot_count, lane_count)

    result = prior_share
    emb_relay = lax.all_to_all(
        relay_pieces(embeddings), "member", split_axis=0, concat_axis=0, tiled=True
    )
    emb_near = lax.all_to_all(
        deliver_pieces(emb_relay), "member", split_axis=0, concat_axis=0, tiled=True
    )
    emb_far = extended(emb_blocks[cross_pick], (("group", 0),), 1)
    key_rows = jnp.concatenate([embeddings, near_keys(emb_near), far_keys(emb_far)], axis=0)
    weights = kernel_weights(embeddings, key_rows, allowed)
    for iteration in range(ITERS):
        lab_blocks = labels.reshape(block_count, block_rows, classes)
        lab_relay = lax.all_to_all(
            relay_pieces(labels), "member", split_axis=0, concat_axis=0, tiled=True
        )
        lab_near = lax.all_to_all(
            deliver_pieces(lab_relay), "member", split_axis=0, concat_axis=0, tiled=True
        )
        lab_far = extended(lab_blocks[cross_pick], (("group", 0),), 1)
        key_labels = jnp.concatenate([labels, near_keys(lab_near), far_keys(lab_far)], axis=0)
        result = sharpen(weights, key_labels, prior_share)
        labels = result.astype(jnp.bfloat16)
    return result * classes


MESH = pl.DeviceIdType.MESH


def partner_of(member, mask, member_count):
    bit = 1
    while bit < member_count:
        if mask & bit:
            member = member + bit - 2 * bit * (member // bit % 2)
        bit *= 2
    return member


def same(left, right):
    gap = left - right
    return 1 - jnp.minimum(gap * gap, 1)


def direct_kernel(
    member_count, group_count,
    owners, blocks, cross, emb_hbm, prior_hbm, links_hbm, out,
    emb, share, links, emb_send, emb_recv, lab_low, lab_high, send_low, send_high, recv_low, recv_high,
    sums, sum_send, sum_recv, keys_ref, scores, weights, mix,
    load_sem, send_sem, recv_sem,
):
    group = lax.axis_index("group")
    me = lax.axis_index("member")
    block_count, _, features = emb.shape
    rows = block_count * BR
    in_slots = owners.shape[0]
    below = (group + group_count - 1) % group_count
    above = (group + 1) % group_count
    group_blocks = 2 if block_count % 2 == 0 else 1
    width = group_blocks * BR
    chunks = rows // width
    slots = 2 + member_count - 1
    partners = [partner_of(me, mask, member_count) for mask in range(1, member_count)]
    targets = [(above, me), (below, me)] + [(group, p) for p in partners]
    masks = sorted(range(1, member_count), key=lambda mask: (mask == 1, (mask >> 1).bit_count(), mask & 1))
    sending = [1 + mask for mask in masks] + [0, 1]

    labs, lab_sends, lab_recvs = (lab_low, lab_high), (send_low, send_high), (recv_low, recv_high)
    split = lab_low.shape[1]
    heights = (split, lab_high.shape[1])
    bands = (slice(0, split), slice(split, split + heights[1]))

    def lanes_of(c):
        return pl.ds(pl.multiple_of(c * width, width), width)

    emb_load = pltpu.make_async_copy(emb_hbm, emb, load_sem.at[0])
    prior_load = pltpu.make_async_copy(prior_hbm, share, load_sem.at[1])
    links_load = pltpu.make_async_copy(links_hbm, links, load_sem.at[2])
    emb_load.start()
    prior_load.start()
    links_load.start()

    barrier = pltpu.get_barrier_semaphore()
    for target in targets:
        pl.semaphore_signal(barrier, inc=1, device_id=target, device_id_type=MESH)

    picks = [cross[0, above], cross[1, below]]
    names = [jnp.int32(in_slots), jnp.int32(in_slots + 1)]
    for p in partners:
        pick = jnp.int32(0)
        name = jnp.int32(-1)
        for k in range(in_slots):
            pick += same(owners[k, p], me) * blocks[k, p]
            name += same(owners[k, me], p) * (k + 1)
        picks.append(pick)
        names.append(name)

    def copy_of(kind, s):
        sides = [(emb_send, emb_recv)]
        for stage in range(ITERS):
            sides += [(lab_sends[h].at[stage], lab_recvs[h].at[stage]) for h in (0, 1)]
        sides.append((sum_send, sum_recv))
        src, dst = sides[kind]
        return pltpu.make_async_remote_copy(
            src_ref=src.at[s], dst_ref=dst.at[s],
            send_sem=send_sem.at[kind, s], recv_sem=recv_sem.at[kind, s],
            device_id=targets[s], device_id_type=MESH,
        )

    def kind_of(stage, half):
        return 1 + 2 * stage + half

    sum_kind = 1 + 2 * ITERS

    emb_load.wait()
    pl.semaphore_wait(barrier, slots)
    for s in sending:
        emb_send[s] = emb[picks[s]]
        copy_of(0, s).start()

    def put_labels(half, c, value):
        value = value.astype(jnp.bfloat16)
        for b in range(group_blocks):
            labs[half][c * group_blocks + b] = value[:, b * BR:(b + 1) * BR]

    def send_labels(stage, half):
        for s in sending:
            lab_sends[half][stage, s] = labs[half][picks[s]]
            copy_of(kind_of(stage, half), s).start()

    prior_load.wait()

    def first_labels(c, _):
        lanes = lanes_of(c)
        value = share[:, lanes]
        value = value / jnp.sum(value, axis=0, keepdims=True)
        share[:, lanes] = value
        for half in (0, 1):
            put_labels(half, c, value[bands[half]])
        return _

    lax.fori_loop(0, chunks, first_labels, 0)
    send_labels(0, 0)
    send_labels(0, 1)
    links_load.wait()

    def score_of(keys):
        value = lax.dot_general(
            keys, emb[...].reshape(rows, features), (((1,), (1,)), ((), ())), preferred_element_type=jnp.float32
        )
        return value * features ** (-0.5)

    def own_scores(b, _):
        span = pl.ds(pl.multiple_of(b * BR, BR), BR)
        value = score_of(emb[b])
        key_ids = lax.broadcasted_iota(jnp.int32, (BR, rows), 0) + b * BR
        row_ids = lax.broadcasted_iota(jnp.int32, (BR, rows), 1)
        scores[span, :] = jnp.where(key_ids != row_ids, value, -jnp.inf)
        return _

    lax.fori_loop(0, rows // BR, own_scores, 0)
    for s in range(slots):
        bias = jnp.max(jnp.where(links[...] == names[s], 0.0, -jnp.inf), axis=0, keepdims=True)
        copy_of(0, s).wait_recv()
        scores[rows + s * BR:rows + (s + 1) * BR, :] = score_of(emb_recv[s]) + bias

    def soften(b, _):
        lanes = pl.ds(pl.multiple_of(b * BR, BR), BR)
        value = scores[:, lanes]
        powers = jnp.exp(value - jnp.max(value, axis=0, keepdims=True))
        total = jnp.sum(powers, axis=0, keepdims=True)
        weights[:, lanes] = (powers * (1.0 / total)).astype(jnp.bfloat16)
        return _

    lax.fori_loop(0, rows // BR, soften, 0)

    def own_mix(c, _):
        lanes = lanes_of(c)
        for half in (0, 1):
            keys = jnp.concatenate([labs[half][b] for b in range(block_count)], axis=1)
            mix[bands[half], lanes] = jnp.dot(
                keys, weights[:rows, lanes], preferred_element_type=jnp.float32
            )
        return _

    def squared_of(total, half, lanes):
        mixed = MIXING * total + (1.0 - MIXING) * share[bands[half], lanes]
        return mixed * mixed

    spans = [(0, 3)] + [(s, min(s + 2, slots)) for s in range(3, slots, 2)]

    def neighbour_mix(stage, half, finish):
        for first, last in spans:
            for s in range(first, last):
                copy_of(kind_of(stage, half), s).wait_recv()
                block = lab_recvs[half][stage, s]
                if stage > 0:
                    if half == 0:
                        copy_of(sum_kind, s).wait_recv()
                    scale = 1.0 / sum_recv[s][:1]
                    block = (block.astype(jnp.float32) * scale).astype(jnp.bfloat16)
                keys_ref[:heights[half], (s - first) * BR:(s - first + 1) * BR] = block

            def arrived(c, _, first=first, last=last):
                lanes = lanes_of(c)
                total = mix[bands[half], lanes] + jnp.dot(
                    keys_ref[:heights[half], :(last - first) * BR],
                    weights[rows + first * BR:rows + last * BR, lanes],
                    preferred_element_type=jnp.float32,
                )
                if last < slots:
                    mix[bands[half], lanes] = total
                else:
                    finish(c, lanes, squared_of(total, half, lanes))
                return _

            lax.fori_loop(0, chunks, arrived, 0)

    def put_sums(half, c, squared):
        part = jnp.sum(squared, axis=0, keepdims=True)
        for b in range(group_blocks):
            value = jnp.broadcast_to(part[:, b * BR:(b + 1) * BR], (8, BR))
            at = c * group_blocks + b
            sums[at] = value if half == 0 else sums[at] + value

    def middle(half):
        def finish(c, lanes, squared):
            mix[bands[half], lanes] = squared
            put_labels(half, c, squared)
            put_sums(half, c, squared)

        return finish

    def own_labels(c, _):
        lanes = lanes_of(c)
        parts = [sums[c * group_blocks + b][:1] for b in range(group_blocks)]
        scale = 1.0 / jnp.concatenate(parts, axis=1)
        for half in (0, 1):
            put_labels(half, c, mix[bands[half], lanes] * scale)
        return _

    for stage in range(ITERS - 1):
        lax.fori_loop(0, chunks, own_mix, 0)
        for half in (0, 1):
            neighbour_mix(stage, half, middle(half))
            if half == 1:
                for s in sending:
                    sum_send[s] = sums[picks[s]]
                    copy_of(sum_kind, s).start()
            send_labels(stage + 1, half)
        lax.fori_loop(0, chunks, own_labels, 0)

    def last_low(c, lanes, squared):
        mix[bands[0], lanes] = squared
        put_sums(0, c, squared)

    def last_high(c, lanes, squared):
        put_sums(1, c, squared)
        parts = [sums[c * group_blocks + b][:1] for b in range(group_blocks)]
        scale = 1.0 / jnp.concatenate(parts, axis=1)
        out[bands[0], lanes] = mix[bands[0], lanes] * scale
        out[bands[1], lanes] = squared * scale

    lax.fori_loop(0, chunks, own_mix, 0)
    neighbour_mix(ITERS - 1, 0, last_low)
    neighbour_mix(ITERS - 1, 1, last_high)
    for kind in range(sum_kind + 1):
        for s in range(slots):
            copy_of(kind, s).wait_send()


def direct_body(embeddings, prior, source_member, source_block, cross_block, row_links):
    member_count = lax.axis_size("member")
    group_count = lax.axis_size("group")
    rows, features = embeddings.shape
    classes = prior.shape[1]
    slots = 2 + member_count - 1
    keys = rows + slots * BR
    split = -(-classes // 32) * 16
    any_space = pl.BlockSpec(memory_space=pl.ANY)
    smem = pl.BlockSpec(memory_space=pltpu.SMEM)
    bf16, f32 = jnp.bfloat16, jnp.float32
    sharp = pl.pallas_call(
        functools.partial(direct_kernel, member_count, group_count),
        out_shape=pltpu.VMEM((classes, rows), f32),
        in_specs=[smem] * 3 + [any_space] * 3,
        out_specs=pl.BlockSpec(memory_space=pltpu.VMEM),
        scratch_shapes=[
            pltpu.VMEM((rows // BR, BR, features), bf16),
            pltpu.VMEM((classes, rows), f32),
            pltpu.VMEM((row_links.shape[1], rows), jnp.int32),
            pltpu.VMEM((slots, BR, features), bf16),
            pltpu.VMEM((slots, BR, features), bf16),
            pltpu.VMEM((rows // BR, split, BR), bf16),
            pltpu.VMEM((rows // BR, classes - split, BR), bf16),
            pltpu.VMEM((ITERS, slots, split, BR), bf16),
            pltpu.VMEM((ITERS, slots, classes - split, BR), bf16),
            pltpu.VMEM((ITERS, slots, split, BR), bf16),
            pltpu.VMEM((ITERS, slots, classes - split, BR), bf16),
            pltpu.VMEM((rows // BR, 8, BR), f32),
            pltpu.VMEM((slots, 8, BR), f32),
            pltpu.VMEM((slots, 8, BR), f32),
            pltpu.VMEM((split, 3 * BR), bf16),
            pltpu.VMEM((keys, rows), f32),
            pltpu.VMEM((keys, rows), bf16),
            pltpu.VMEM((classes, rows), f32),
            pltpu.SemaphoreType.DMA((3,)),
            pltpu.SemaphoreType.DMA((2 * ITERS + 2, slots)),
            pltpu.SemaphoreType.DMA((2 * ITERS + 2, slots)),
        ],
        compiler_params=pltpu.CompilerParams(
            collective_id=0, has_side_effects=True, vmem_limit_bytes=60 * 2**20
        ),
    )(
        source_member[0].T, source_block[0].T, cross_block[:, 0, :].T,
        embeddings.reshape(rows // BR, BR, features), prior.T, row_links.T,
    )
    return sharp.T * classes


def solution(mesh):
    member_count = mesh.shape["member"]
    direct = member_count & (member_count - 1) == 0 and member_count - 1 <= SERVE_CAP
    body = direct_body if direct else relay_body
    placed = (
        P(("group", "member"), None),
        P(("group", "member"), None),
        P("group", None, None),
        P("group", None, None),
        P(None, "member", None),
        P(("group", "member"), None),
    )
    return jax.shard_map(
        body, mesh=mesh, in_specs=placed, out_specs=P(("group", "member"), None), check_vma=False
    )
```

```python
import functools

import jax
import jax.numpy as jnp
from jax import lax
from jax.experimental import pallas as pl
from jax.experimental.pallas import tpu as pltpu
from jax.sharding import PartitionSpec as P

BR = 128
SERVE_CAP = 7
ITERS = 2


MIXING = 0.8


def extended(value, sides, width):
    for axis, dim in sides:
        size, length = (lax.axis_size(axis), value.shape[dim])
        up = [(i, (i + 1) % size) for i in range(size)]
        down = [(j, i) for i, j in up]
        last = lax.slice_in_dim(value, length - width, length, axis=dim)
        first = lax.slice_in_dim(value, 0, width, axis=dim)
        before = lax.ppermute(last, axis, up)
        after = lax.ppermute(first, axis, down)
        value = jnp.concatenate([before, value, after], axis=dim)
    return value


def allowed_mask(row_links, near_total, slot_total, row_count, block_rows):
    slot_ids = jnp.arange(slot_total, dtype=jnp.int32)
    slot_hits = jnp.any(row_links[:, :, None] == slot_ids[None, None, :], axis=1)
    near_mask = jnp.tile(slot_hits[:, :near_total], (1, block_rows))
    far_mask = jnp.repeat(slot_hits[:, near_total:], block_rows, axis=1)
    row_ids = lax.broadcasted_iota(jnp.int32, (row_count, row_count), 0)
    col_ids = lax.broadcasted_iota(jnp.int32, (row_count, row_count), 1)
    local_mask = row_ids != col_ids
    return jnp.concatenate([local_mask, near_mask, far_mask], axis=1)


def kernel_weights(queries, key_rows, allowed):
    features = queries.shape[1]
    scores = lax.dot_general(
        queries, key_rows, (((1,), (1,)), ((), ())), preferred_element_type=jnp.float32
    )
    scores = scores * features ** (-0.5)
    scores = jnp.where(allowed, scores, -jnp.inf)
    highest = jnp.max(scores, axis=1, keepdims=True)
    powers = jnp.where(allowed, jnp.exp(scores - highest), 0.0)
    return (powers / jnp.sum(powers, axis=1, keepdims=True)).astype(jnp.bfloat16)


def sharpen(weights, key_labels, prior_share):
    mixed = (
        MIXING * jnp.dot(weights, key_labels, preferred_element_type=jnp.float32)
        + (1.0 - MIXING) * prior_share
    )
    squared = mixed * mixed
    return squared / jnp.sum(squared, axis=1, keepdims=True)


def near_keys(delivered):
    return delivered.reshape(-1, delivered.shape[-1])


def far_keys(padded):
    return jnp.concatenate([padded[0], padded[-1]], axis=0)


def relay_body(embeddings, prior, source_member, source_block, cross_block, row_links):
    member_count = lax.axis_size("member")
    group_count = lax.axis_size("group")
    group_index = lax.axis_index("group")
    member_index = lax.axis_index("member")
    row_count, features = embeddings.shape
    classes = prior.shape[1]
    block_rows = BR
    block_count = row_count // block_rows
    piece_rows = block_rows // member_count
    owners = source_member[0]
    slot_count = owners.shape[1]
    flat_owner = owners.reshape(-1)
    flat_block = source_block[0].reshape(-1)
    order_ids = jnp.arange(flat_owner.shape[0], dtype=jnp.int32)
    earlier = (flat_owner[:, None] == flat_owner[None, :]) & (
        order_ids[None, :] < order_ids[:, None]
    )
    rank_ids = jnp.sum(earlier.astype(jnp.int32), axis=1)
    serve_ids = jnp.arange(SERVE_CAP, dtype=jnp.int32)
    serving = (flat_owner[None, :] == member_index) & (rank_ids[None, :] == serve_ids[:, None])
    served_blocks = jnp.sum(jnp.where(serving, flat_block[None, :], 0), axis=1)
    relay_member = lax.broadcasted_iota(jnp.int32, (member_count, piece_rows, SERVE_CAP), 0)
    relay_row = lax.broadcasted_iota(jnp.int32, (member_count, piece_rows, SERVE_CAP), 1)
    relay_rows = (
        served_blocks[None, None, :] * block_rows + relay_member * piece_rows + relay_row
    ).reshape(-1)
    owner_grid = owners.reshape(member_count, 1, slot_count)
    rank_grid = rank_ids.reshape(member_count, 1, slot_count)
    piece_grid = lax.broadcasted_iota(jnp.int32, (member_count, piece_rows, slot_count), 1)
    deliver_rows = (
        owner_grid * (piece_rows * SERVE_CAP) + piece_grid * SERVE_CAP + rank_grid
    ).reshape(-1)
    below_group = (group_index + group_count - 1) % group_count
    above_group = (group_index + 1) % group_count
    cross_pick = jnp.stack([cross_block[below_group, 0, 1], cross_block[above_group, 0, 0]])
    allowed = allowed_mask(
        row_links, slot_count, slot_count + cross_block.shape[2], row_count, block_rows
    )
    prior_share = prior / jnp.sum(prior, axis=1, keepdims=True)
    labels = prior_share.astype(jnp.bfloat16)
    emb_blocks = embeddings.reshape(block_count, block_rows, features)

    def relay_pieces(flat_rows):
        return jnp.take(flat_rows, relay_rows, axis=0).reshape(
            member_count, piece_rows, SERVE_CAP, flat_rows.shape[-1]
        )

    def deliver_pieces(received):
        lane_count = received.shape[-1]
        picked = jnp.take(received.reshape(-1, lane_count), deliver_rows, axis=0)
        return picked.reshape(member_count, piece_rows, slot_count, lane_count)

    result = prior_share
    emb_relay = lax.all_to_all(
        relay_pieces(embeddings), "member", split_axis=0, concat_axis=0, tiled=True
    )
    emb_near = lax.all_to_all(
        deliver_pieces(emb_relay), "member", split_axis=0, concat_axis=0, tiled=True
    )
    emb_far = extended(emb_blocks[cross_pick], (("group", 0),), 1)
    key_rows = jnp.concatenate([embeddings, near_keys(emb_near), far_keys(emb_far)], axis=0)
    weights = kernel_weights(embeddings, key_rows, allowed)
    for iteration in range(ITERS):
        lab_blocks = labels.reshape(block_count, block_rows, classes)
        lab_relay = lax.all_to_all(
            relay_pieces(labels), "member", split_axis=0, concat_axis=0, tiled=True
        )
        lab_near = lax.all_to_all(
            deliver_pieces(lab_relay), "member", split_axis=0, concat_axis=0, tiled=True
        )
        lab_far = extended(lab_blocks[cross_pick], (("group", 0),), 1)
        key_labels = jnp.concatenate([labels, near_keys(lab_near), far_keys(lab_far)], axis=0)
        result = sharpen(weights, key_labels, prior_share)
        labels = result.astype(jnp.bfloat16)
    return result * classes


MESH = pl.DeviceIdType.MESH


def partner_of(member, mask, member_count):
    bit = 1
    while bit < member_count:
        if mask & bit:
            member = member + bit - 2 * bit * (member // bit % 2)
        bit *= 2
    return member


def same(left, right):
    gap = left - right
    return 1 - jnp.minimum(gap * gap, 1)


def direct_kernel(
    member_count, group_count,
    owners, blocks, cross, emb_hbm, prior_hbm, links_hbm, out,
    emb, share, links, emb_send, emb_recv, lab_low, lab_high, send_low, send_high, recv_low, recv_high,
    sums, sum_send, sum_recv, keys_ref, scores, weights, mix,
    load_sem, send_sem, recv_sem,
):
    group = lax.axis_index("group")
    me = lax.axis_index("member")
    block_count, _, features = emb.shape
    rows = block_count * BR
    in_slots = owners.shape[0]
    below = (group + group_count - 1) % group_count
    above = (group + 1) % group_count
    group_blocks = 2 if block_count % 2 == 0 else 1
    width = group_blocks * BR
    chunks = rows // width
    slots = 2 + member_count - 1
    partners = [partner_of(me, mask, member_count) for mask in range(1, member_count)]
    targets = [(above, me), (below, me)] + [(group, p) for p in partners]
    masks = sorted(range(1, member_count), key=lambda mask: (mask == 1, (mask >> 1).bit_count(), mask & 1))
    sending = [0, 1] + [1 + mask for mask in masks]

    labs, lab_sends, lab_recvs = (lab_low, lab_high), (send_low, send_high), (recv_low, recv_high)
    split = lab_low.shape[1]
    heights = (split, lab_high.shape[1])
    bands = (slice(0, split), slice(split, split + heights[1]))

    def lanes_of(c):
        return pl.ds(pl.multiple_of(c * width, width), width)

    emb_load = pltpu.make_async_copy(emb_hbm, emb, load_sem.at[0])
    prior_load = pltpu.make_async_copy(prior_hbm, share, load_sem.at[1])
    links_load = pltpu.make_async_copy(links_hbm, links, load_sem.at[2])
    emb_load.start()
    prior_load.start()
    links_load.start()

    barrier = pltpu.get_barrier_semaphore()
    for target in targets:
        pl.semaphore_signal(barrier, inc=1, device_id=target, device_id_type=MESH)

    picks = [cross[0, above], cross[1, below]]
    names = [jnp.int32(in_slots), jnp.int32(in_slots + 1)]
    for p in partners:
        pick = jnp.int32(0)
        name = jnp.int32(-1)
        for k in range(in_slots):
            pick += same(owners[k, p], me) * blocks[k, p]
            name += same(owners[k, me], p) * (k + 1)
        picks.append(pick)
        names.append(name)

    def copy_of(kind, s):
        sides = [(emb_send, emb_recv)]
        for stage in range(ITERS):
            sides += [(lab_sends[h].at[stage], lab_recvs[h].at[stage]) for h in (0, 1)]
        sides.append((sum_send, sum_recv))
        src, dst = sides[kind]
        return pltpu.make_async_remote_copy(
            src_ref=src.at[s], dst_ref=dst.at[s],
            send_sem=send_sem.at[kind, s], recv_sem=recv_sem.at[kind, s],
            device_id=targets[s], device_id_type=MESH,
        )

    def kind_of(stage, half):
        return 1 + 2 * stage + half

    sum_kind = 1 + 2 * ITERS

    emb_load.wait()
    pl.semaphore_wait(barrier, slots)
    for s in sending:
        emb_send[s] = emb[picks[s]]
        copy_of(0, s).start()

    def put_labels(half, c, value):
        value = value.astype(jnp.bfloat16)
        for b in range(group_blocks):
            labs[half][c * group_blocks + b] = value[:, b * BR:(b + 1) * BR]

    def send_labels(stage, half):
        for s in sending:
            lab_sends[half][stage, s] = labs[half][picks[s]]
            copy_of(kind_of(stage, half), s).start()

    prior_load.wait()

    def first_labels(c, _):
        lanes = lanes_of(c)
        value = share[:, lanes]
        value = value / jnp.sum(value, axis=0, keepdims=True)
        share[:, lanes] = value
        for half in (0, 1):
            put_labels(half, c, value[bands[half]])
        return _

    lax.fori_loop(0, chunks, first_labels, 0)
    send_labels(0, 0)
    send_labels(0, 1)
    links_load.wait()

    def score_of(keys):
        value = lax.dot_general(
            keys, emb[...].reshape(rows, features), (((1,), (1,)), ((), ())), preferred_element_type=jnp.float32
        )
        return value * features ** (-0.5)

    def own_scores(b, _):
        span = pl.ds(pl.multiple_of(b * BR, BR), BR)
        value = score_of(emb[b])
        key_ids = lax.broadcasted_iota(jnp.int32, (BR, rows), 0) + b * BR
        row_ids = lax.broadcasted_iota(jnp.int32, (BR, rows), 1)
        scores[span, :] = jnp.where(key_ids != row_ids, value, -jnp.inf)
        return _

    lax.fori_loop(0, rows // BR, own_scores, 0)
    for s in range(slots):
        bias = jnp.max(jnp.where(links[...] == names[s], 0.0, -jnp.inf), axis=0, keepdims=True)
        copy_of(0, s).wait_recv()
        scores[rows + s * BR:rows + (s + 1) * BR, :] = score_of(emb_recv[s]) + bias

    def soften(b, _):
        lanes = pl.ds(pl.multiple_of(b * BR, BR), BR)
        value = scores[:, lanes]
        powers = jnp.exp(value - jnp.max(value, axis=0, keepdims=True))
        total = jnp.sum(powers, axis=0, keepdims=True)
        weights[:, lanes] = (powers * (1.0 / total)).astype(jnp.bfloat16)
        return _

    lax.fori_loop(0, rows // BR, soften, 0)

    def own_mix(c, _):
        lanes = lanes_of(c)
        for half in (0, 1):
            keys = jnp.concatenate([labs[half][b] for b in range(block_count)], axis=1)
            mix[bands[half], lanes] = jnp.dot(
                keys, weights[:rows, lanes], preferred_element_type=jnp.float32
            )
        return _

    def squared_of(total, half, lanes):
        mixed = MIXING * total + (1.0 - MIXING) * share[bands[half], lanes]
        return mixed * mixed

    spans = [(0, 3)] + [(s, min(s + 2, slots)) for s in range(3, slots, 2)]

    def neighbour_mix(stage, half, finish):
        for first, last in spans:
            for s in range(first, last):
                copy_of(kind_of(stage, half), s).wait_recv()
                block = lab_recvs[half][stage, s]
                if stage > 0:
                    if half == 0:
                        copy_of(sum_kind, s).wait_recv()
                    scale = 1.0 / sum_recv[s][:1]
                    block = (block.astype(jnp.float32) * scale).astype(jnp.bfloat16)
                keys_ref[:heights[half], (s - first) * BR:(s - first + 1) * BR] = block

            def arrived(c, _, first=first, last=last):
                lanes = lanes_of(c)
                total = mix[bands[half], lanes] + jnp.dot(
                    keys_ref[:heights[half], :(last - first) * BR],
                    weights[rows + first * BR:rows + last * BR, lanes],
                    preferred_element_type=jnp.float32,
                )
                if last < slots:
                    mix[bands[half], lanes] = total
                else:
                    finish(c, lanes, squared_of(total, half, lanes))
                return _

            lax.fori_loop(0, chunks, arrived, 0)

    def put_sums(half, c, squared):
        part = jnp.sum(squared, axis=0, keepdims=True)
        for b in range(group_blocks):
            value = jnp.broadcast_to(part[:, b * BR:(b + 1) * BR], (8, BR))
            at = c * group_blocks + b
            sums[at] = value if half == 0 else sums[at] + value

    def middle(half):
        def finish(c, lanes, squared):
            mix[bands[half], lanes] = squared
            put_labels(half, c, squared)
            put_sums(half, c, squared)

        return finish

    def own_labels(c, _):
        lanes = lanes_of(c)
        parts = [sums[c * group_blocks + b][:1] for b in range(group_blocks)]
        scale = 1.0 / jnp.concatenate(parts, axis=1)
        for half in (0, 1):
            put_labels(half, c, mix[bands[half], lanes] * scale)
        return _

    for stage in range(ITERS - 1):
        lax.fori_loop(0, chunks, own_mix, 0)
        for half in (0, 1):
            neighbour_mix(stage, half, middle(half))
            if half == 1:
                for s in sending:
                    sum_send[s] = sums[picks[s]]
                    copy_of(sum_kind, s).start()
            send_labels(stage + 1, half)
        lax.fori_loop(0, chunks, own_labels, 0)

    def last_low(c, lanes, squared):
        mix[bands[0], lanes] = squared
        put_sums(0, c, squared)

    def last_high(c, lanes, squared):
        put_sums(1, c, squared)
        parts = [sums[c * group_blocks + b][:1] for b in range(group_blocks)]
        scale = 1.0 / jnp.concatenate(parts, axis=1)
        out[bands[0], lanes] = mix[bands[0], lanes] * scale
        out[bands[1], lanes] = squared * scale

    lax.fori_loop(0, chunks, own_mix, 0)
    neighbour_mix(ITERS - 1, 0, last_low)
    neighbour_mix(ITERS - 1, 1, last_high)
    for kind in range(sum_kind + 1):
        for s in range(slots):
            copy_of(kind, s).wait_send()


def direct_body(embeddings, prior, source_member, source_block, cross_block, row_links):
    member_count = lax.axis_size("member")
    group_count = lax.axis_size("group")
    rows, features = embeddings.shape
    classes = prior.shape[1]
    slots = 2 + member_count - 1
    keys = rows + slots * BR
    split = -(-classes // 32) * 16
    any_space = pl.BlockSpec(memory_space=pl.ANY)
    smem = pl.BlockSpec(memory_space=pltpu.SMEM)
    bf16, f32 = jnp.bfloat16, jnp.float32
    sharp = pl.pallas_call(
        functools.partial(direct_kernel, member_count, group_count),
        out_shape=pltpu.VMEM((classes, rows), f32),
        in_specs=[smem] * 3 + [any_space] * 3,
        out_specs=pl.BlockSpec(memory_space=pltpu.VMEM),
        scratch_shapes=[
            pltpu.VMEM((rows // BR, BR, features), bf16),
            pltpu.VMEM((classes, rows), f32),
            pltpu.VMEM((row_links.shape[1], rows), jnp.int32),
            pltpu.VMEM((slots, BR, features), bf16),
            pltpu.VMEM((slots, BR, features), bf16),
            pltpu.VMEM((rows // BR, split, BR), bf16),
            pltpu.VMEM((rows // BR, classes - split, BR), bf16),
            pltpu.VMEM((ITERS, slots, split, BR), bf16),
            pltpu.VMEM((ITERS, slots, classes - split, BR), bf16),
            pltpu.VMEM((ITERS, slots, split, BR), bf16),
            pltpu.VMEM((ITERS, slots, classes - split, BR), bf16),
            pltpu.VMEM((rows // BR, 8, BR), f32),
            pltpu.VMEM((slots, 8, BR), f32),
            pltpu.VMEM((slots, 8, BR), f32),
            pltpu.VMEM((split, 3 * BR), bf16),
            pltpu.VMEM((keys, rows), f32),
            pltpu.VMEM((keys, rows), bf16),
            pltpu.VMEM((classes, rows), f32),
            pltpu.SemaphoreType.DMA((3,)),
            pltpu.SemaphoreType.DMA((2 * ITERS + 2, slots)),
            pltpu.SemaphoreType.DMA((2 * ITERS + 2, slots)),
        ],
        compiler_params=pltpu.CompilerParams(
            collective_id=0, has_side_effects=True, vmem_limit_bytes=60 * 2**20
        ),
    )(
        source_member[0].T, source_block[0].T, cross_block[:, 0, :].T,
        embeddings.reshape(rows // BR, BR, features), prior.T, row_links.T,
    )
    return sharp.T * classes


def solution(mesh):
    member_count = mesh.shape["member"]
    direct = member_count & (member_count - 1) == 0 and member_count - 1 <= SERVE_CAP
    body = direct_body if direct else relay_body
    placed = (
        P(("group", "member"), None),
        P(("group", "member"), None),
        P("group", None, None),
        P("group", None, None),
        P(None, "member", None),
        P(("group", "member"), None),
    )
    return jax.shard_map(
        body, mesh=mesh, in_specs=placed, out_specs=P(("group", "member"), None), check_vma=False
    )
```
